32 devices in a mesh: groups: 2 (over y), seq: 4 (over z), head: 2 (over x), rep: 2 (over core).
Axes of the slice: x: 2, y: 2, z: 4, core: 2. Of those that a mesh axis runs over, the one named last changes fastest.
Arguments:
- queries: bfloat16 [8192, 4096], P(('groups', 'seq', 'rep'), 'head'), parts along dimension 0, may hold values from -6 to 6
- keys: bfloat16 [8192, 4096], P(('groups', 'seq', 'rep'), 'head'), parts along dimension 0, may hold values from -6 to 6
- values: bfloat16 [8192, 4096], P(('groups', 'seq', 'rep'), 'head'), parts along dimension 0, may hold values from -6 to 6
- d_out: bfloat16 [8192, 4096], P(('groups', 'seq', 'rep'), 'head'), parts along dimension 0, may hold values from -6 to 6
- doc_lengths: int32 [16], P('groups'), parts along dimension 0, may hold values from 1 to 2048, 4096 in all
- gain: float32 [4096], P('head'), may hold values from 0.25 to 1.75
Outputs:
- mixed: bfloat16 [8192, 4096], P(('groups', 'seq', 'rep'), 'head'), parts along dimension 0
- grad_queries: bfloat16 [8192, 4096], P(('groups', 'seq', 'rep'), 'head'), parts along dimension 0
- grad_keys: bfloat16 [8192, 4096], P(('groups', 'seq', 'rep'), 'head'), parts along dimension 0
- grad_values: bfloat16 [8192, 4096], P(('groups', 'seq', 'rep'), 'head'), parts along dimension 0
- grad_gain: float32 [2, 4096], P('groups', 'head'), parts along dimension 0
The draws below stay inside these ranges and needn't reach their ends.
There are 2 independent parts, one for each index of `groups`. The reference program is written for one: setup_inputs(seed, part) draws one part's arguments, and reference() takes and returns one part's arrays. A program takes and returns all parts, laid end to end along the dimension named above; an argument that names none is the same for every part. Nothing has to cross between parts.
Inputs may be any that keep to these rules, and one draw needn't show every extreme that they name: `doc_lengths`: the entries sum to 4096, and the largest is exactly half of 4096.
All inputs are finite; a program needn't handle non-finite values.
Results may differ from the reference program's by a relative error of at most 0.0059.
Values sent between devices are 32-bit elements; how exact they have to be, the bound alone decides.
A program may use at most 128 MiB of HBM per device.

```python
import math
import jax
import jax.numpy as jnp
import numpy as np
from jax import lax

HEADS = 32
DH = 128
NDOC = 8
BLOCK = 512
LEN = 4096


def levels(own_key, shape, split, smallest, top_value):
    factor_of = 1.0
    for position, shards_of in split:
        draws = jax.random.uniform(jax.random.fold_in(jax.random.fold_in(own_key, 6), position), (shards_of,), jnp.float32, smallest / len(split), top_value / len(split))
        factor_of = factor_of * jnp.repeat(jnp.exp(draws), shape[position] // shards_of).reshape((-1,) + (1,) * (len(shape) - 1 - position))
    return factor_of


def split_up(amount, total, most, slope):
    portions = [(1 << 20) // math.isqrt(standing ** slope) + 1 for standing in range(2, amount + 1)]
    surplus, holding = total - most - (amount - 1), [1] * (amount - 1)
    while surplus > 0:
        candidates = [i for i in range(amount - 1) if holding[i] < most]
        whole, remaining = sum([portions[i] for i in candidates]), surplus
        for i in candidates:
            extra = min(most - holding[i], max(1, remaining * portions[i] // whole), surplus)
            holding[i] = holding[i] + extra
            surplus = surplus - extra
    return np.array([most] + holding)


def ragged_sizes(key, number_of, total, most, lean):
    if number_of == 2:
        one = jax.random.randint(key, (), max(1, total - most), min(most, total - 1) + 1)
        return jnp.stack([one, total - one])
    sizes = jnp.asarray(split_up(number_of, total, most, lean), jnp.int32)
    twos = (number_of - 1) // 2
    donor, receiver = sizes[1:1 + 2 * twos:2], sizes[2:2 + 2 * twos:2]
    margin = jnp.minimum(donor - 1, most - receiver)
    passed = jax.random.randint(jax.random.fold_in(key, 1), (twos,), 0, 1 << 20) % (margin + 1)
    sizes = sizes.at[1:1 + 2 * twos:2].set(donor - passed).at[2:2 + 2 * twos:2].set(receiver + passed)
    return sizes[jax.random.permutation(jax.random.fold_in(key, 2), number_of)]


def bell_draw(rng, dims, spread, most, cuts=(), held_as=jnp.bfloat16):
    array = spread * jax.random.normal(rng, dims, jnp.float32)
    if cuts:
        array = array * levels(rng, dims, cuts, -0.22, 0.18)
    return jnp.clip(array, -most, most).astype(held_as)


def setup_inputs(seed: int = 0, part: int = 0) -> dict:
    splits = jax.random.split(jax.random.key(seed), 7)
    part_splits = jax.random.split(jax.random.fold_in(splits[6], part), 7)
    queries = bell_draw(part_splits[0], (LEN, HEADS * DH), 1.0, 6.0, ((0, 8), (1, 2)))
    keys = bell_draw(part_splits[1], (LEN, HEADS * DH), 1.0, 6.0, ((0, 8), (1, 2)))
    values = bell_draw(part_splits[2], (LEN, HEADS * DH), 1.0, 6.0, ((0, 8), (1, 2)))
    d_out = bell_draw(part_splits[3], (LEN, HEADS * DH), 1.0, 6.0, ((0, 8), (1, 2)))
    doc_lengths = ragged_sizes(part_splits[4], NDOC, LEN, LEN // 2, 2).astype(jnp.int32)
    gain = jnp.clip(1.0 + 0.15 * jax.random.normal(splits[5], (HEADS * DH,), jnp.float32), 0.25, 1.75)
    return {"queries": queries, "keys": keys, "values": values, "d_out": d_out, "doc_lengths": doc_lengths, "gain": gain}


def doc_index(doc_ends, places):
    return lax.optimization_barrier(jnp.sum((doc_ends[None, :] <= places[:, None]).astype(jnp.int32), axis=1))

def rounded(value):
    return lax.optimization_barrier(value.astype(jnp.bfloat16)).astype(jnp.float32)

def same_doc(block_docs):
    places = jnp.arange(block_docs.shape[0])
    return (block_docs[:, None] == block_docs[None, :]) & (places[:, None] >= places[None, :])

def forward_block(state_in, inputs):
    query_blk, key_blk, value_blk, block_docs, prior_doc = inputs
    scores = jnp.einsum('thd,shd->hts', query_blk, key_blk) / DH
    weights = rounded(jnp.where(same_doc(block_docs)[None], scores, 0.0))
    inner_sum = jnp.einsum('hts,shd->thd', weights, value_blk)
    carried = jnp.einsum('thd,hde->the', query_blk, rounded(state_in)) / DH
    output = inner_sum + jnp.where((block_docs == prior_doc)[:, None, None], carried, 0.0)
    tail_mask = (block_docs == block_docs[-1]).astype(jnp.float32)
    local_sum = jnp.einsum('thd,the->hde', key_blk * tail_mask[:, None, None], value_blk)
    renewed = local_sum + jnp.where(block_docs[-1] == prior_doc, state_in, 0.0)
    return (renewed, (output, state_in))

def backward_block(grad_state, inputs):
    query_blk, key_blk, value_blk, grad_blk, block_docs, prior_doc, next_doc, state_in = inputs
    doc_mask = same_doc(block_docs)[None]
    scores = jnp.einsum('thd,shd->hts', query_blk, key_blk) / DH
    weights = rounded(jnp.where(doc_mask, scores, 0.0))
    grad_scores = jnp.einsum('the,she->hts', grad_blk, value_blk)
    grad_weights = rounded(jnp.where(doc_mask, grad_scores, 0.0))
    grad_query = jnp.einsum('hts,shd->thd', grad_weights, key_blk) / DH
    grad_key = jnp.einsum('hts,thd->shd', grad_weights, query_blk) / DH
    grad_value = jnp.einsum('hts,the->she', weights, grad_blk)
    from_state = jnp.einsum('the,hde->thd', grad_blk, rounded(state_in)) / DH
    grad_query = grad_query + jnp.where((block_docs == prior_doc)[:, None, None], from_state, 0.0)
    later_mask = (block_docs == next_doc)[:, None, None]
    state_low = rounded(grad_state)
    grad_key = grad_key + jnp.where(later_mask, jnp.einsum('she,hde->shd', value_blk, state_low) / DH, 0.0)
    grad_value = grad_value + jnp.where(later_mask, jnp.einsum('shd,hde->she', key_blk, state_low) / DH, 0.0)
    head_mask = (block_docs == block_docs[0]).astype(jnp.float32)
    local_sum = jnp.einsum('thd,the->hde', query_blk * head_mask[:, None, None], grad_blk)
    renewed = local_sum + jnp.where(block_docs[0] == next_doc, grad_state, 0.0)
    return (renewed, (grad_query, grad_key, grad_value))

def reference(queries, keys, values, d_out, doc_lengths, gain):
    blocks = LEN // BLOCK
    shaped = (blocks, BLOCK, HEADS, DH)
    gains = gain.astype(jnp.float32).reshape(HEADS, DH)
    doc_ends = jnp.cumsum(doc_lengths).astype(jnp.int32)
    docs = doc_index(doc_ends, jnp.arange(LEN, dtype=jnp.int32))
    doc_blks = docs.reshape(blocks, BLOCK)
    priors = jnp.concatenate([doc_index(doc_ends, jnp.full((1,), -1, jnp.int32)), doc_blks[:-1, -1]])
    nexts = jnp.concatenate([doc_blks[1:, 0], doc_index(doc_ends, jnp.full((1,), LEN, jnp.int32))])
    query_blks = queries.astype(jnp.float32).reshape(shaped)
    key_blks = keys.astype(jnp.float32).reshape(shaped)
    value_blks = values.astype(jnp.float32).reshape(shaped)
    zero_state = jnp.zeros((HEADS, DH, DH), jnp.float32)
    final_state, (outputs, states) = lax.scan(forward_block, zero_state, (query_blks, key_blks, value_blks, doc_blks, priors))
    mean_sq = lax.optimization_barrier(jnp.mean(outputs * outputs, axis=-1, keepdims=True))
    inverse = lax.rsqrt(mean_sq + 1e-05)
    normed = outputs * inverse
    mixed = (normed * gains).astype(jnp.bfloat16)
    grad_out = d_out.astype(jnp.float32).reshape(shaped)
    gain_terms = lax.optimization_barrier(jnp.sum(grad_out * normed, axis=(0, 1)))
    grad_normed = grad_out * gains
    grad_attn = rounded(inverse * (grad_normed - normed * lax.optimization_barrier(jnp.mean(grad_normed * normed, axis=-1, keepdims=True))))
    final_grad, (grad_q, grad_k, grad_v) = lax.scan(backward_block, zero_state, (query_blks, key_blks, value_blks, grad_attn, doc_blks, priors, nexts, states), reverse=True)
    flat = (LEN, HEADS * DH)
    grad_gain = (gain_terms / math.sqrt(LEN)).reshape(1, HEADS * DH)
    return (mixed.reshape(flat), grad_q.astype(jnp.bfloat16).reshape(flat), grad_k.astype(jnp.bfloat16).reshape(flat), grad_v.astype(jnp.bfloat16).reshape(flat), grad_gain)
```

```python
import functools
import math

import jax
import jax.numpy as jnp
from jax import lax
from jax.experimental import pallas as pl
from jax.experimental.pallas import tpu as pltpu
from jax.sharding import PartitionSpec as P

DH = 128
HALF = 256
MESH = pl.DeviceIdType.MESH
F32 = jnp.float32
BF16 = jnp.bfloat16


def nn(a, b):
    return lax.dot_general(a, b, (((1,), (0,)), ((), ())), preferred_element_type=F32)


def nt(a, b):
    return lax.dot_general(a, b, (((1,), (1,)), ((), ())), preferred_element_type=F32)


def tn(a, b):
    return lax.dot_general(a, b, (((0,), (0,)), ((), ())), preferred_element_type=F32)


def kernel(
    heads, tokens, seqs, reps, ndoc,
    lens, gain, q_hbm, k_hbm, v_hbm, d_hbm,
    mix_hbm, gq_hbm, gk_hbm, gv_hbm, ggain,
    qs, ks, vs, ds, acc, w_top, w_bot, gs, mask, prior_m, next_m, tail_m, head_m,
    fout, fin, bout, bin_, sb, gsb, ob, gslots,
    in_sem, out_sem, fsend, frecv, bsend, brecv, gsend, grecv,
):
    n = seqs * reps
    rank = lax.axis_index("seq") * reps + lax.axis_index("rep")
    total = n * tokens
    first = rank * tokens
    top = slice(0, HALF)
    bot = slice(HALF, 2 * HALF)

    def device(other):
        return {"seq": lax.div(other, reps), "rep": lax.rem(other, reps)}

    def cols(h):
        return pl.ds(pl.multiple_of(h * DH, DH), DH)

    def load(i, hbm, buf, h):
        return pltpu.make_async_copy(hbm.at[:, cols(h)], buf.at[h], in_sem.at[i, h])

    def store(i, hbm, h):
        return pltpu.make_async_copy(ob.at[i, h], hbm.at[:, cols(h)], out_sem.at[i, h])

    def each(fn):
        lax.fori_loop(0, heads, lambda h, c: (fn(h), c)[1], 0)

    def start_kv(h):
        load(0, k_hbm, ks, h).start()
        load(1, v_hbm, vs, h).start()

    def start_qd(h):
        load(2, q_hbm, qs, h).start()
        load(3, d_hbm, ds, h).start()

    each(start_kv)
    each(start_qd)
    barrier = pltpu.get_barrier_semaphore()
    for o in range(1, n):
        pl.semaphore_signal(barrier, inc=1, device_id=device(lax.rem(rank + o, n)), device_id_type=MESH)

    ends = []
    run = jnp.int32(0)
    for i in range(ndoc):
        run = run + lens[i]
        ends.append(run)

    def doc_of(place):
        return sum((jnp.where(e <= place, 1, 0) for e in ends))

    before, after = doc_of(first - 1), doc_of(first + tokens)
    doc_first, doc_last = doc_of(first), doc_of(first + tokens - 1)
    col = lax.broadcasted_iota(jnp.int32, (tokens, DH), 0)
    doc_col = doc_of(col + first)
    prior_m[...] = jnp.where(doc_col == before, 1.0, 0.0)
    next_m[...] = jnp.where(doc_col == after, 1.0, 0.0)
    tail_m[...] = jnp.where(doc_col == doc_last, 1.0, 0.0).astype(BF16)
    head_m[...] = jnp.where(doc_col == doc_first, 1.0, 0.0).astype(BF16)
    place_row = lax.broadcasted_iota(jnp.int32, (8, tokens), 1)
    doc_row = doc_of(place_row + first)
    for j in range(tokens // DH):
        lanes = slice(j * DH, (j + 1) * DH)
        u = place_row[0:1, lanes]
        keep = (doc_col == doc_row[0:1, lanes]) & (col >= u)
        mask[:, lanes] = jnp.where(keep, 1.0 / DH, 0.0)
    pass_f = jnp.where(doc_last == before, 1.0, 0.0)
    pass_b = jnp.where(doc_first == after, 1.0, 0.0)

    @pl.when(rank == 0)
    def _():
        fin[...] = jnp.zeros_like(fin)

    @pl.when(rank == n - 1)
    def _():
        bin_[...] = jnp.zeros_like(bin_)

    def local(h):
        load(0, k_hbm, ks, h).wait()
        load(1, v_hbm, vs, h).wait()
        fout[h] = tn(ks[h] * tail_m[...], vs[h])

    each(local)
    pl.semaphore_wait(barrier, n - 1)

    def fcopy(h):
        return pltpu.make_async_remote_copy(
            src_ref=fout.at[h], dst_ref=fin.at[h], send_sem=fsend.at[h], recv_sem=frecv.at[h],
            device_id=device(jnp.minimum(rank + 1, n - 1)), device_id_type=MESH,
        )

    def bcopy(h):
        return pltpu.make_async_remote_copy(
            src_ref=bout.at[h], dst_ref=bin_.at[h], send_sem=bsend.at[h], recv_sem=brecv.at[h],
            device_id=device(jnp.maximum(rank - 1, 0)), device_id_type=MESH,
        )

    def gcopy(o):
        return pltpu.make_async_remote_copy(
            src_ref=gslots.at[rank], dst_ref=gslots.at[rank], send_sem=gsend.at[o], recv_sem=grecv.at[rank],
            device_id=device(lax.rem(rank + o, n)), device_id_type=MESH,
        )

    def scores(h):
        load(2, q_hbm, qs, h).wait()
        w_top[h] = (nt(qs[h, top], ks[h, top]) * mask[top, top]).astype(BF16)
        w_bot[h] = (nt(qs[h, bot], ks[h]) * mask[bot]).astype(BF16)
        acc[h, top] = nn(w_top[h], vs[h, top])
        acc[h, bot] = nn(w_bot[h], vs[h])

    def forward(h):
        @pl.when(rank > 0)
        def _():
            fcopy(h).wait_recv()

        fout[h] = fout[h] + pass_f * fin[h]

        @pl.when(rank < n - 1)
        def _():
            fcopy(h).start()

        load(3, d_hbm, ds, h).wait()
        sb[h] = (fin[h] * (1.0 / DH)).astype(BF16)
        attn = acc[h] + prior_m[...] * nn(qs[h], sb[h])
        inverse = lax.rsqrt(jnp.mean(attn * attn, axis=-1, keepdims=True) + 1e-5)
        normed = attn * inverse
        gains = gain[pl.ds(h, 1), :]
        ob[0, h] = (normed * gains).astype(BF16)
        store(0, mix_hbm, h).start()
        d = ds[h].astype(F32)
        terms = d * normed
        gslots[rank, pl.ds(h, 1), :] = jnp.sum(terms, axis=0, keepdims=True)
        g = d * gains
        inner = jnp.mean(g * normed, axis=-1, keepdims=True)
        grad = (inverse * (g - normed * inner)).astype(BF16)
        gs[h] = grad
        bout[h] = tn(qs[h] * head_m[...], grad)

    def backward(h):
        @pl.when(rank < n - 1)
        def _():
            bcopy(h).wait_recv()

        bout[h] = bout[h] + pass_b * bin_[h]

        @pl.when(rank > 0)
        def _():
            bcopy(h).start()

        gsb[h] = (bin_[h] * (1.0 / DH)).astype(BF16)

    def grads(h):
        gt = (nt(gs[h, top], vs[h, top]) * mask[top, top]).astype(BF16)
        gb = (nt(gs[h, bot], vs[h]) * mask[bot]).astype(BF16)
        from_state = prior_m[...] * nt(gs[h], sb[h])
        ob[1, h, top] = (nn(gt, ks[h, top]) + from_state[top]).astype(BF16)
        ob[1, h, bot] = (nn(gb, ks[h]) + from_state[bot]).astype(BF16)
        store(1, gq_hbm, h).start()
        later = next_m[...] * nt(vs[h], gsb[h])
        low = tn(gb, qs[h, bot])
        ob[2, h, top] = (tn(gt, qs[h, top]) + low[top] + later[top]).astype(BF16)
        ob[2, h, bot] = (low[bot] + later[bot]).astype(BF16)
        store(2, gk_hbm, h).start()
        later = next_m[...] * nn(ks[h], gsb[h])
        low = tn(w_bot[h], gs[h, bot])
        ob[3, h, top] = (tn(w_top[h], gs[h, top]) + low[top] + later[top]).astype(BF16)
        ob[3, h, bot] = (low[bot] + later[bot]).astype(BF16)
        store(3, gv_hbm, h).start()

    d1 = lax.div(rank * heads, n - 1)
    d3 = d1 + 1 + lax.div((n - 1 - rank) * heads, n - 1)
    d4 = d3 + 1

    def stage(i, delay, fn):
        @pl.when((i >= delay) & (i < delay + heads))
        def _():
            fn(i - delay)

    def step(i, c):
        stage(i, 0, scores)
        stage(i, d1, forward)

        @pl.when(i == d1 + heads - 1)
        def _():
            for o in range(1, n):
                gcopy(o).start()

        stage(i, d3, backward)
        stage(i, d4, grads)
        return c

    lax.fori_loop(0, d4 + heads, step, 0)

    for o in range(1, n):
        src = lax.rem(rank + n - o, n)
        pltpu.make_async_remote_copy(
            src_ref=gslots.at[src], dst_ref=gslots.at[src], send_sem=gsend.at[o], recv_sem=grecv.at[src],
            device_id=device(src), device_id_type=MESH,
        ).wait_recv()
        gcopy(o).wait_send()
    summed = gslots[0]
    for i in range(1, n):
        summed = summed + gslots[i]
    ggain[...] = summed * (1.0 / math.sqrt(total))

    def finish(h):
        @pl.when(rank < n - 1)
        def _():
            fcopy(h).wait_send()

        @pl.when(rank > 0)
        def _():
            bcopy(h).wait_send()

        store(0, mix_hbm, h).wait()
        store(1, gq_hbm, h).wait()
        store(2, gk_hbm, h).wait()
        store(3, gv_hbm, h).wait()

    each(finish)


def shards(queries, keys, values, d_out, doc_lengths, gain):
    tokens, width = queries.shape
    heads = width // DH
    seqs, reps = lax.axis_size("seq"), lax.axis_size("rep")
    n = seqs * reps
    slab = pltpu.VMEM((heads, tokens, DH), BF16)
    state = pltpu.VMEM((heads, DH, DH), F32)
    state_low = pltpu.VMEM((heads, DH, DH), BF16)
    dma = pltpu.SemaphoreType.DMA
    big = jax.ShapeDtypeStruct((tokens, width), BF16)
    hbm = pl.BlockSpec(memory_space=pl.ANY)
    vmem = pl.BlockSpec(memory_space=pltpu.VMEM)
    out = pl.pallas_call(
        functools.partial(kernel, heads, tokens, seqs, reps, doc_lengths.shape[0]),
        out_shape=(big, big, big, big, jax.ShapeDtypeStruct((heads, DH), F32)),
        in_specs=[pl.BlockSpec(memory_space=pltpu.SMEM), vmem, hbm, hbm, hbm, hbm],
        out_specs=(hbm, hbm, hbm, hbm, vmem),
        scratch_shapes=[
            slab, slab, slab, slab,
            pltpu.VMEM((heads, tokens, DH), F32),
            pltpu.VMEM((heads, HALF, HALF), BF16),
            pltpu.VMEM((heads, HALF, 2 * HALF), BF16),
            slab,
            pltpu.VMEM((tokens, tokens), F32),
            pltpu.VMEM((tokens, DH), F32),
            pltpu.VMEM((tokens, DH), F32),
            pltpu.VMEM((tokens, DH), BF16),
            pltpu.VMEM((tokens, DH), BF16),
            state, state, state, state, state_low, state_low,
            pltpu.VMEM((4, heads, tokens, DH), BF16),
            pltpu.VMEM((n, heads, DH), F32),
            dma((4, heads)), dma((4, heads)),
            dma((heads,)), dma((heads,)), dma((heads,)), dma((heads,)),
            dma((n,)), dma((n,)),
        ],
        compiler_params=pltpu.CompilerParams(
            collective_id=0, has_side_effects=True, vmem_limit_bytes=52 << 20
        ),
    )(doc_lengths, gain.reshape(heads, DH), queries, keys, values, d_out)
    return (*out[:4], out[4].reshape(1, width))


def solution(mesh):
    token = P(("groups", "seq", "rep"), "head")
    return jax.shard_map(
        shards,
        mesh=mesh,
        in_specs=(token, token, token, token, P("groups"), P("head")),
        out_specs=(token, token, token, token, P("groups", "head")),
        check_vma=False,
    )
```

```python
import functools
import math

import jax
import jax.numpy as jnp
from jax import lax
from jax.experimental import pallas as pl
from jax.experimental.pallas import tpu as pltpu
from jax.sharding import PartitionSpec as P

DH = 128
HALF = 256
F_BASE, F_HOP, G_LAG, G_HOP = 9, 5, 2, 5
MESH = pl.DeviceIdType.MESH
F32 = jnp.float32
BF16 = jnp.bfloat16


def nn(a, b):
    return lax.dot_general(a, b, (((1,), (0,)), ((), ())), preferred_element_type=F32)


def nt(a, b):
    return lax.dot_general(a, b, (((1,), (1,)), ((), ())), preferred_element_type=F32)


def tn(a, b):
    return lax.dot_general(a, b, (((0,), (0,)), ((), ())), preferred_element_type=F32)


def kernel(
    heads, tokens, seqs, reps, ndoc,
    lens_hbm, gain_hbm, q_hbm, k_hbm, v_hbm, d_hbm,
    mix, gq, gk, gv, ggain,
    lens, gain, qs, ks, vs, ds, acc, w_top, w_bot, gs, mask, prior_m, next_m, tail_m, head_m,
    fown, fpart, fin, fout, frel, fstate,
    bown, bpart, bin_, bout, brel, bstate,
    sb, gsb, gslots,
    in_sem, small_sem, fsem, bsem, gsend, grecv,
):
    n = seqs * reps
    chip, core = lax.axis_index("seq"), lax.axis_index("rep")
    rank = chip * reps + core
    total = n * tokens
    first = rank * tokens
    top = slice(0, HALF)
    bot = slice(HALF, 2 * HALF)

    def device(other):
        return {"seq": lax.div(other, reps), "rep": lax.rem(other, reps)}

    def cols(h):
        return pl.ds(pl.multiple_of(h * DH, DH), DH)

    def load(i, hbm, buf, h):
        return pltpu.make_async_copy(hbm.at[:, cols(h)], buf.at[h], in_sem.at[i, h])

    def each(fn):
        lax.fori_loop(0, heads, lambda h, c: (fn(h), c)[1], 0)

    def start_kv(h):
        load(0, k_hbm, ks, h).start()
        load(1, v_hbm, vs, h).start()

    def start_qd(h):
        load(2, q_hbm, qs, h).start()
        load(3, d_hbm, ds, h).start()

    lens_copy = pltpu.make_async_copy(lens_hbm, lens, small_sem.at[0])
    gain_copy = pltpu.make_async_copy(gain_hbm, gain, small_sem.at[1])
    lens_copy.start()
    gain_copy.start()
    each(start_kv)
    each(start_qd)
    barrier = pltpu.get_barrier_semaphore()
    for o in range(1, n):
        pl.semaphore_signal(barrier, inc=1, device_id=device(lax.rem(rank + o, n)), device_id_type=MESH)

    lens_copy.wait()
    gain_copy.wait()

    ends = []
    run = jnp.int32(0)
    for i in range(ndoc):
        run = run + lens[i]
        ends.append(run)

    def doc_of(place):
        return sum((jnp.where(e <= place, 1, 0) for e in ends))

    before, after = doc_of(first - 1), doc_of(first + tokens)
    doc_first, doc_last = doc_of(first), doc_of(first + tokens - 1)
    col = lax.broadcasted_iota(jnp.int32, (tokens, DH), 0)
    doc_col = doc_of(col + first)
    prior_m[...] = jnp.where(doc_col == before, 1.0, 0.0)
    next_m[...] = jnp.where(doc_col == after, 1.0, 0.0)
    tail_m[...] = jnp.where(doc_col == doc_last, 1.0, 0.0).astype(BF16)
    head_m[...] = jnp.where(doc_col == doc_first, 1.0, 0.0).astype(BF16)
    place_row = lax.broadcasted_iota(jnp.int32, (8, tokens), 1)
    doc_row = doc_of(place_row + first)
    for j in range(tokens // DH):
        lanes = slice(j * DH, (j + 1) * DH)
        u = place_row[0:1, lanes]
        keep = (doc_col == doc_row[0:1, lanes]) & (col >= u)
        mask[:, lanes] = jnp.where(keep, 1.0 / DH, 0.0)

    def carries(one, other):
        return jnp.where(doc_of(one) == doc_of(other), 1.0, 0.0)

    base = chip * reps * tokens
    flags_f = [carries(base + i * tokens - 1, base + (i + 1) * tokens - 1) for i in range(2)]
    flags_b = [carries(base + i * tokens, base + (i + 1) * tokens) for i in (1, 0)]

    @pl.when(chip == 0)
    def _():
        fin[...] = jnp.zeros_like(fin)

    @pl.when(chip == seqs - 1)
    def _():
        bin_[...] = jnp.zeros_like(bin_)

    other_core = {"rep": 1 - core}

    def remote(src, dst, sems, kind, p, where):
        return pltpu.make_async_remote_copy(
            src_ref=src.at[p] if kind else src, dst_ref=dst.at[p],
            send_sem=sems.at[kind, 0, p], recv_sem=sems.at[kind, 1, p],
            device_id=where, device_id_type=MESH,
        )

    class Chain:
        def __init__(self, own, part, arrived, out, rel, state, sems, low, late, flags, ends, onward):
            self.own, self.part, self.arrived, self.out = own, part, arrived, out
            self.rel, self.state, self.sems, self.low = rel, state, sems, low
            f0, f1 = flags
            self.c_own, self.c_part = jnp.where(late, 1.0, f1), jnp.where(late, f1, 1.0)
            self.c_in = f0 * f1
            self.own_part, self.own_in = jnp.where(late, 1.0, 0.0), jnp.where(late, f0, 1.0)
            self.rel_own, self.rel_in = jnp.where(late, 0.0, 1.0), jnp.where(late, 1.0, f0)
            self.is_first, self.is_last = ends
            self.onward = onward

        def to_partner(self, h):
            p = lax.div(h, 2)
            return remote(self.own.at[h], self.part, self.sems, 0, p, other_core)

        def to_next(self, p):
            return remote(self.out, self.arrived, self.sems, 1, p, self.onward)

        def relay(self, p):
            return remote(self.rel, self.state, self.sems, 2, p, other_core)

        def send_own(self, h):
            @pl.when(lax.rem(h, 2) != core)
            def _():
                self.to_partner(h).start()

        def step(self, h):
            @pl.when(lax.rem(h, 2) == core)
            def _():
                p = lax.div(h, 2)
                self.to_partner(h).wait_recv()

                @pl.when(jnp.logical_not(self.is_first))
                def _():
                    self.to_next(p).wait_recv()

                own, part, came = self.own[h], self.part[p], self.arrived[p]

                @pl.when(jnp.logical_not(self.is_last))
                def _():
                    self.out[p] = self.c_own * own + self.c_part * part + self.c_in * came
                    self.to_next(p).start()

                self.rel[p] = self.rel_own * own + self.rel_in * came
                self.relay(p).start()
                self.low[h] = ((self.own_part * part + self.own_in * came) * (1.0 / DH)).astype(BF16)

        def take(self, h):
            @pl.when(lax.rem(h, 2) != core)
            def _():
                p = lax.div(h, 2)
                self.relay(p).wait_recv()
                self.low[h] = (self.state[p] * (1.0 / DH)).astype(BF16)

        def finish(self, h):
            p = lax.div(h, 2)

            @pl.when(lax.rem(h, 2) != core)
            def _():
                self.to_partner(h).wait_send()

            @pl.when(lax.rem(h, 2) == core)
            def _():
                self.relay(p).wait_send()

                @pl.when(jnp.logical_not(self.is_last))
                def _():
                    self.to_next(p).wait_send()

    ahead = Chain(
        fown, fpart, fin, fout, frel, fstate, fsem, sb, core == 1, flags_f,
        (chip == 0, chip == seqs - 1), {"seq": jnp.minimum(chip + 1, seqs - 1)},
    )
    back = Chain(
        bown, bpart, bin_, bout, brel, bstate, bsem, gsb, core == 0, flags_b,
        (chip == seqs - 1, chip == 0), {"seq": jnp.maximum(chip - 1, 0)},
    )

    pl.semaphore_wait(barrier, n - 1)

    def local(h):
        load(0, k_hbm, ks, h).wait()
        load(1, v_hbm, vs, h).wait()
        fown[h] = tn(ks[h] * tail_m[...], vs[h])
        ahead.send_own(h)

    def gcopy(o):
        return pltpu.make_async_remote_copy(
            src_ref=gslots.at[rank], dst_ref=gslots.at[rank], send_sem=gsend.at[o], recv_sem=grecv.at[rank],
            device_id=device(lax.rem(rank + o, n)), device_id_type=MESH,
        )

    def scores(h):
        load(2, q_hbm, qs, h).wait()
        w_top[h] = (nt(qs[h, top], ks[h, top]) * mask[top, top]).astype(BF16)
        w_bot[h] = (nt(qs[h, bot], ks[h]) * mask[bot]).astype(BF16)
        acc[h, top] = nn(w_top[h], vs[h, top])
        acc[h, bot] = nn(w_bot[h], vs[h])

    def forward(h):
        ahead.take(h)
        load(3, d_hbm, ds, h).wait()
        attn = acc[h] + prior_m[...] * nn(qs[h], sb[h])
        inverse = lax.rsqrt(jnp.mean(attn * attn, axis=-1, keepdims=True) + 1e-5)
        normed = attn * inverse
        gains = gain[pl.ds(h, 1), :]
        mix[:, cols(h)] = (normed * gains).astype(BF16)
        d = ds[h].astype(F32)
        terms = d * normed
        gslots[rank, pl.ds(h, 1), :] = jnp.sum(terms, axis=0, keepdims=True)
        g = d * gains
        inner = jnp.mean(g * normed, axis=-1, keepdims=True)
        grad = (inverse * (g - normed * inner)).astype(BF16)
        gs[h] = grad
        bown[h] = tn(qs[h] * head_m[...], grad)
        back.send_own(h)

    def grads(h):
        back.take(h)
        gt = (nt(gs[h, top], vs[h, top]) * mask[top, top]).astype(BF16)
        gb = (nt(gs[h, bot], vs[h]) * mask[bot]).astype(BF16)
        from_state = prior_m[...] * nt(gs[h], sb[h])
        gq[top, cols(h)] = (nn(gt, ks[h, top]) + from_state[top]).astype(BF16)
        gq[bot, cols(h)] = (nn(gb, ks[h]) + from_state[bot]).astype(BF16)
        later = next_m[...] * nt(vs[h], gsb[h])
        low = tn(gb, qs[h, bot])
        gk[top, cols(h)] = (tn(gt, qs[h, top]) + low[top] + later[top]).astype(BF16)
        gk[bot, cols(h)] = (low[bot] + later[bot]).astype(BF16)
        later = next_m[...] * nn(ks[h], gsb[h])
        low = tn(w_bot[h], gs[h, bot])
        gv[top, cols(h)] = (tn(w_top[h], gs[h, top]) + low[top] + later[top]).astype(BF16)
        gv[bot, cols(h)] = (low[bot] + later[bot]).astype(BF16)

    def ahead_done(i):
        due = F_BASE + F_HOP * chip
        spread = jnp.where(chip == 0, i - 2, lax.div(jnp.maximum(i - due + 1, 0) * 5, 9))
        spread = jnp.minimum(spread, i)
        return jnp.clip(jnp.maximum(spread, i - 2 * heads + 1), 0, heads)

    def back_done(i):
        due = 2 * heads + G_LAG + G_HOP * (seqs - 1 - chip)
        return jnp.clip(i + 1 - jnp.minimum(due, 3 * heads), 0, heads)

    def stage(i, delay, fn):
        @pl.when((i >= delay) & (i < delay + heads))
        def _():
            fn(i - delay)

    def chain_steps(chain, low, high):
        lax.fori_loop(low, high, lambda h, c: (chain.step(h), c)[1], 0)

    def step(i, c):
        stage(i, 0, local)
        stage(i, heads, scores)
        chain_steps(ahead, ahead_done(i - 1), ahead_done(i))
        stage(i, 2 * heads, forward)

        @pl.when(i == 3 * heads - 1)
        def _():
            for o in range(1, n):
                gcopy(o).start()

        chain_steps(back, back_done(i - 1), back_done(i))
        stage(i, 3 * heads, grads)
        return c

    lax.fori_loop(0, 4 * heads, step, 0)

    for o in range(1, n):
        src = lax.rem(rank + n - o, n)
        pltpu.make_async_remote_copy(
            src_ref=gslots.at[src], dst_ref=gslots.at[src], send_sem=gsend.at[o], recv_sem=grecv.at[src],
            device_id=device(src), device_id_type=MESH,
        ).wait_recv()
        gcopy(o).wait_send()
    summed = gslots[0]
    for i in range(1, n):
        summed = summed + gslots[i]
    ggain[...] = summed * (1.0 / math.sqrt(total))

    def finish(h):
        ahead.finish(h)
        back.finish(h)

    each(finish)


def shards(queries, keys, values, d_out, doc_lengths, gain):
    tokens, width = queries.shape
    heads = width // DH
    seqs, reps = lax.axis_size("seq"), lax.axis_size("rep")
    n = seqs * reps
    slab = pltpu.VMEM((heads, tokens, DH), BF16)
    state = pltpu.VMEM((heads, DH, DH), F32)
    state_low = pltpu.VMEM((heads, DH, DH), BF16)
    half = pltpu.VMEM((heads // 2, DH, DH), F32)
    dma = pltpu.SemaphoreType.DMA
    big = jax.ShapeDtypeStruct((tokens, width), BF16)
    hbm = pl.BlockSpec(memory_space=pltpu.HBM)
    vmem = pl.BlockSpec(memory_space=pltpu.VMEM)
    out = pl.pallas_call(
        functools.partial(kernel, heads, tokens, seqs, reps, doc_lengths.shape[0]),
        out_shape=(big, big, big, big, jax.ShapeDtypeStruct((heads, DH), F32)),
        in_specs=[hbm] * 6,
        out_specs=(vmem,) * 5,
        scratch_shapes=[
            pltpu.SMEM(doc_lengths.shape, jnp.int32),
            pltpu.VMEM((heads, DH), F32),
            slab, slab, slab, slab,
            pltpu.VMEM((heads, tokens, DH), F32),
            pltpu.VMEM((heads, HALF, HALF), BF16),
            pltpu.VMEM((heads, HALF, 2 * HALF), BF16),
            slab,
            pltpu.VMEM((tokens, tokens), F32),
            pltpu.VMEM((tokens, DH), F32),
            pltpu.VMEM((tokens, DH), F32),
            pltpu.VMEM((tokens, DH), BF16),
            pltpu.VMEM((tokens, DH), BF16),
            state, half, half, half, half, half,
            state, half, half, half, half, half,
            state_low, state_low,
            pltpu.VMEM((n, heads, DH), F32),
            dma((4, heads)), dma((2,)), dma((3, 2, heads // 2)), dma((3, 2, heads // 2)),
            dma((n,)), dma((n,)),
        ],
        compiler_params=pltpu.CompilerParams(
            collective_id=0, has_side_effects=True, vmem_limit_bytes=44 << 20
        ),
    )(doc_lengths, gain.reshape(heads, DH), queries, keys, values, d_out)
    return (*out[:4], out[4].reshape(1, width))


def solution(mesh):
    token = P(("groups", "seq", "rep"), "head")
    return jax.shard_map(
        shards,
        mesh=mesh,
        in_specs=(token, token, token, token, P("groups"), P("head")),
        out_specs=(token, token, token, token, P("groups", "head")),
        check_vma=False,
    )
```

```python
import functools
import math

import jax
import jax.numpy as jnp
from jax import lax
from jax.experimental import pallas as pl
from jax.experimental.pallas import tpu as pltpu
from jax.sharding import PartitionSpec as P

DH = 128
HALF = 256
F_BASE, F_HOP, G_LAG, G_HOP = 4, 4, 1, 3
MESH = pl.DeviceIdType.MESH
F32 = jnp.float32
BF16 = jnp.bfloat16


def nn(a, b):
    return lax.dot_general(a, b, (((1,), (0,)), ((), ())), preferred_element_type=F32)


def nt(a, b):
    return lax.dot_general(a, b, (((1,), (1,)), ((), ())), preferred_element_type=F32)


def tn(a, b):
    return lax.dot_general(a, b, (((0,), (0,)), ((), ())), preferred_element_type=F32)


def kernel(
    heads, tokens, seqs, reps, ndoc,
    lens_hbm, gain_hbm, q_hbm, k_hbm, v_hbm, d_hbm,
    mix, gq, gk, gv, ggain,
    lens, gain, qs, ks, vs, ds, acc, w_top, w_bot, gs, mask, prior_m, next_m, tail_m, head_m,
    fown, fpart, fin, fout, frel, fstate,
    bown, bpart, bin_, bout, brel, bstate,
    sb, gsb, gslots,
    in_sem, small_sem, fsem, bsem, gsend, grecv,
):
    n = seqs * reps
    chip, core = lax.axis_index("seq"), lax.axis_index("rep")
    rank = chip * reps + core
    total = n * tokens
    first = rank * tokens
    top = slice(0, HALF)
    bot = slice(HALF, 2 * HALF)

    def device(other):
        return {"seq": lax.div(other, reps), "rep": lax.rem(other, reps)}

    def cols(h):
        return pl.ds(pl.multiple_of(h * DH, DH), DH)

    def load(i, hbm, buf, h):
        return pltpu.make_async_copy(hbm.at[:, cols(h)], buf.at[h], in_sem.at[i, h])

    def each(fn):
        lax.fori_loop(0, heads, lambda h, c: (fn(h), c)[1], 0)

    def start_kv(h):
        load(0, k_hbm, ks, h).start()
        load(1, v_hbm, vs, h).start()

    def start_qd(h):
        load(2, q_hbm, qs, h).start()
        load(3, d_hbm, ds, h).start()

    lens_copy = pltpu.make_async_copy(lens_hbm, lens, small_sem.at[0])
    gain_copy = pltpu.make_async_copy(gain_hbm, gain, small_sem.at[1])
    lens_copy.start()
    gain_copy.start()
    each(start_kv)
    each(start_qd)
    barrier = pltpu.get_barrier_semaphore()
    for o in range(1, n):
        pl.semaphore_signal(barrier, inc=1, device_id=device(lax.rem(rank + o, n)), device_id_type=MESH)

    lens_copy.wait()
    gain_copy.wait()

    ends = []
    run = jnp.int32(0)
    for i in range(ndoc):
        run = run + lens[i]
        ends.append(run)

    def doc_of(place):
        return sum((jnp.where(e <= place, 1, 0) for e in ends))

    before, after = doc_of(first - 1), doc_of(first + tokens)
    doc_first, doc_last = doc_of(first), doc_of(first + tokens - 1)
    col = lax.broadcasted_iota(jnp.int32, (tokens, DH), 0)
    doc_col = doc_of(col + first)
    prior_m[...] = jnp.where(doc_col == before, 1.0, 0.0)
    next_m[...] = jnp.where(doc_col == after, 1.0, 0.0)
    tail_m[...] = jnp.where(doc_col == doc_last, 1.0, 0.0).astype(BF16)
    head_m[...] = jnp.where(doc_col == doc_first, 1.0, 0.0).astype(BF16)
    place_row = lax.broadcasted_iota(jnp.int32, (8, tokens), 1)
    doc_row = doc_of(place_row + first)
    for j in range(tokens // DH):
        lanes = slice(j * DH, (j + 1) * DH)
        u = place_row[0:1, lanes]
        keep = (doc_col == doc_row[0:1, lanes]) & (col >= u)
        mask[:, lanes] = jnp.where(keep, 1.0 / DH, 0.0)

    def carries(one, other):
        return jnp.where(doc_of(one) == doc_of(other), 1.0, 0.0)

    base = chip * reps * tokens
    flags_f = [carries(base + i * tokens - 1, base + (i + 1) * tokens - 1) for i in range(2)]
    flags_b = [carries(base + i * tokens, base + (i + 1) * tokens) for i in (1, 0)]

    @pl.when(chip == 0)
    def _():
        fin[...] = jnp.zeros_like(fin)

    @pl.when(chip == seqs - 1)
    def _():
        bin_[...] = jnp.zeros_like(bin_)

    other_core = {"rep": 1 - core}

    def remote(src, dst, sems, kind, p, where):
        return pltpu.make_async_remote_copy(
            src_ref=src.at[p] if kind else src, dst_ref=dst.at[p],
            send_sem=sems.at[kind, 0, p], recv_sem=sems.at[kind, 1, p],
            device_id=where, device_id_type=MESH,
        )

    class Chain:
        def __init__(self, own, part, arrived, out, rel, state, sems, low, late, flags, ends, onward):
            self.own, self.part, self.arrived, self.out = own, part, arrived, out
            self.rel, self.state, self.sems, self.low = rel, state, sems, low
            f0, f1 = flags
            self.c_own, self.c_part = jnp.where(late, 1.0, f1), jnp.where(late, f1, 1.0)
            self.c_in = f0 * f1
            self.own_part, self.own_in = jnp.where(late, 1.0, 0.0), jnp.where(late, f0, 1.0)
            self.rel_own, self.rel_in = jnp.where(late, 0.0, 1.0), jnp.where(late, 1.0, f0)
            self.is_first, self.is_last = ends
            self.onward = onward

        def to_partner(self, h):
            p = lax.div(h, 2)
            return remote(self.own.at[h], self.part, self.sems, 0, p, other_core)

        def to_next(self, p):
            return remote(self.out, self.arrived, self.sems, 1, p, self.onward)

        def relay(self, p):
            return remote(self.rel, self.state, self.sems, 2, p, other_core)

        def send_own(self, h):
            @pl.when(lax.rem(h, 2) != core)
            def _():
                self.to_partner(h).start()

        def step(self, h):
            @pl.when(lax.rem(h, 2) == core)
            def _():
                p = lax.div(h, 2)
                self.to_partner(h).wait_recv()

                @pl.when(jnp.logical_not(self.is_first))
                def _():
                    self.to_next(p).wait_recv()

                own, part, came = self.own[h], self.part[p], self.arrived[p]

                self.rel[p] = self.rel_own * own + self.rel_in * came
                self.relay(p).start()
                @pl.when(jnp.logical_not(self.is_last))
                def _():
                    self.out[p] = self.c_own * own + self.c_part * part + self.c_in * came
                    self.to_next(p).start()

                self.low[h] = ((self.own_part * part + self.own_in * came) * (1.0 / DH)).astype(BF16)

        def take(self, h):
            @pl.when(lax.rem(h, 2) != core)
            def _():
                p = lax.div(h, 2)
                self.relay(p).wait_recv()
                self.low[h] = (self.state[p] * (1.0 / DH)).astype(BF16)

        def finish(self, h):
            p = lax.div(h, 2)

            @pl.when(lax.rem(h, 2) != core)
            def _():
                self.to_partner(h).wait_send()

            @pl.when(lax.rem(h, 2) == core)
            def _():
                self.relay(p).wait_send()

                @pl.when(jnp.logical_not(self.is_last))
                def _():
                    self.to_next(p).wait_send()

    ahead = Chain(
        fown, fpart, fin, fout, frel, fstate, fsem, sb, core == 1, flags_f,
        (chip == 0, chip == seqs - 1), {"seq": jnp.minimum(chip + 1, seqs - 1)},
    )
    back = Chain(
        bown, bpart, bin_, bout, brel, bstate, bsem, gsb, core == 0, flags_b,
        (chip == seqs - 1, chip == 0), {"seq": jnp.maximum(chip - 1, 0)},
    )

    pl.semaphore_wait(barrier, n - 1)

    def local(h):
        load(0, k_hbm, ks, h).wait()
        load(1, v_hbm, vs, h).wait()
        fown[h] = tn(ks[h] * tail_m[...], vs[h])
        ahead.send_own(h)

    def gcopy(o):
        return pltpu.make_async_remote_copy(
            src_ref=gslots.at[rank], dst_ref=gslots.at[rank], send_sem=gsend.at[o], recv_sem=grecv.at[rank],
            device_id=device(lax.rem(rank + o, n)), device_id_type=MESH,
        )

    def scores(h):
        load(2, q_hbm, qs, h).wait()
        w_top[h] = (nt(qs[h, top], ks[h, top]) * mask[top, top]).astype(BF16)
        w_bot[h] = (nt(qs[h, bot], ks[h]) * mask[bot]).astype(BF16)
        acc[h, top] = nn(w_top[h], vs[h, top])
        acc[h, bot] = nn(w_bot[h], vs[h])

    def forward(h):
        ahead.take(h)
        load(3, d_hbm, ds, h).wait()
        attn = acc[h] + prior_m[...] * nn(qs[h], sb[h])
        inverse = lax.rsqrt(jnp.mean(attn * attn, axis=-1, keepdims=True) + 1e-5)
        normed = attn * inverse
        gains = gain[pl.ds(h, 1), :]
        mix[:, cols(h)] = (normed * gains).astype(BF16)
        d = ds[h].astype(F32)
        terms = d * normed
        gslots[rank, pl.ds(h, 1), :] = jnp.sum(terms, axis=0, keepdims=True)
        g = d * gains
        inner = jnp.mean(g * normed, axis=-1, keepdims=True)
        grad = (inverse * (g - normed * inner)).astype(BF16)
        gs[h] = grad
        bown[h] = tn(qs[h] * head_m[...], grad)
        back.send_own(h)

    def grads(h):
        back.take(h)
        gt = (nt(gs[h, top], vs[h, top]) * mask[top, top]).astype(BF16)
        gb = (nt(gs[h, bot], vs[h]) * mask[bot]).astype(BF16)
        from_state = prior_m[...] * nt(gs[h], sb[h])
        gq[top, cols(h)] = (nn(gt, ks[h, top]) + from_state[top]).astype(BF16)
        gq[bot, cols(h)] = (nn(gb, ks[h]) + from_state[bot]).astype(BF16)
        later = next_m[...] * nt(vs[h], gsb[h])
        low = tn(gb, qs[h, bot])
        gk[top, cols(h)] = (tn(gt, qs[h, top]) + low[top] + later[top]).astype(BF16)
        gk[bot, cols(h)] = (low[bot] + later[bot]).astype(BF16)
        later = next_m[...] * nn(ks[h], gsb[h])
        low = tn(w_bot[h], gs[h, bot])
        gv[top, cols(h)] = (tn(w_top[h], gs[h, top]) + low[top] + later[top]).astype(BF16)
        gv[bot, cols(h)] = (low[bot] + later[bot]).astype(BF16)

    def ahead_done(i):
        due = F_BASE + F_HOP * chip
        spread = jnp.where(chip == 0, i - 2, lax.div(jnp.maximum(i - due + 1, 0) * 5, 9))
        spread = jnp.minimum(spread, i)
        return jnp.clip(jnp.maximum(spread, i - 2 * heads + 1), 0, heads)

    def back_done(i):
        due = 2 * heads + G_LAG + G_HOP * (seqs - 1 - chip)
        return jnp.clip(i + 1 - jnp.minimum(due, 3 * heads), 0, heads)

    def stage(i, delay, fn):
        @pl.when((i >= delay) & (i < delay + heads))
        def _():
            fn(i - delay)

    def chain_steps(chain, low, high):
        lax.fori_loop(low, high, lambda h, c: (chain.step(h), c)[1], 0)

    def step(i, c):
        stage(i, 0, local)
        stage(i, heads, scores)
        chain_steps(ahead, ahead_done(i - 1), ahead_done(i))
        stage(i, 2 * heads, forward)

        @pl.when(i == 3 * heads - 1)
        def _():
            for o in range(1, n):
                gcopy(o).start()

        chain_steps(back, back_done(i - 1), back_done(i))
        stage(i, 3 * heads, grads)
        return c

    lax.fori_loop(0, 4 * heads, step, 0)

    for o in range(1, n):
        src = lax.rem(rank + n - o, n)
        pltpu.make_async_remote_copy(
            src_ref=gslots.at[src], dst_ref=gslots.at[src], send_sem=gsend.at[o], recv_sem=grecv.at[src],
            device_id=device(src), device_id_type=MESH,
        ).wait_recv()
        gcopy(o).wait_send()
    summed = gslots[0]
    for i in range(1, n):
        summed = summed + gslots[i]
    ggain[...] = summed * (1.0 / math.sqrt(total))

    def finish(h):
        ahead.finish(h)
        back.finish(h)

    each(finish)


def shards(queries, keys, values, d_out, doc_lengths, gain):
    tokens, width = queries.shape
    heads = width // DH
    seqs, reps = lax.axis_size("seq"), lax.axis_size("rep")
    n = seqs * reps
    slab = pltpu.VMEM((heads, tokens, DH), BF16)
    state = pltpu.VMEM((heads, DH, DH), F32)
    state_low = pltpu.VMEM((heads, DH, DH), BF16)
    half = pltpu.VMEM((heads // 2, DH, DH), F32)
    dma = pltpu.SemaphoreType.DMA
    big = jax.ShapeDtypeStruct((tokens, width), BF16)
    hbm = pl.BlockSpec(memory_space=pltpu.HBM)
    vmem = pl.BlockSpec(memory_space=pltpu.VMEM)
    out = pl.pallas_call(
        functools.partial(kernel, heads, tokens, seqs, reps, doc_lengths.shape[0]),
        out_shape=(big, big, big, big, jax.ShapeDtypeStruct((heads, DH), F32)),
        in_specs=[hbm] * 6,
        out_specs=(vmem,) * 5,
        scratch_shapes=[
            pltpu.SMEM(doc_lengths.shape, jnp.int32),
            pltpu.VMEM((heads, DH), F32),
            slab, slab, slab, slab,
            pltpu.VMEM((heads, tokens, DH), F32),
            pltpu.VMEM((heads, HALF, HALF), BF16),
            pltpu.VMEM((heads, HALF, 2 * HALF), BF16),
            slab,
            pltpu.VMEM((tokens, tokens), F32),
            pltpu.VMEM((tokens, DH), F32),
            pltpu.VMEM((tokens, DH), F32),
            pltpu.VMEM((tokens, DH), BF16),
            pltpu.VMEM((tokens, DH), BF16),
            state, half, half, half, half, half,
            state, half, half, half, half, half,
            state_low, state_low,
            pltpu.VMEM((n, heads, DH), F32),
            dma((4, heads)), dma((2,)), dma((3, 2, heads // 2)), dma((3, 2, heads // 2)),
            dma((n,)), dma((n,)),
        ],
        compiler_params=pltpu.CompilerParams(
            collective_id=0, has_side_effects=True, vmem_limit_bytes=44 << 20
        ),
    )(doc_lengths, gain.reshape(heads, DH), queries, keys, values, d_out)
    return (*out[:4], out[4].reshape(1, width))


def solution(mesh):
    token = P(("groups", "seq", "rep"), "head")
    return jax.shard_map(
        shards,
        mesh=mesh,
        in_specs=(token, token, token, token, P("groups"), P("head")),
        out_specs=(token, token, token, token, P("groups", "head")),
        check_vma=False,
    )
```
